256 devices in a mesh: tensor: 8 (over y, core), store: 32 (over z, x).
Axes of the slice: x: 4, y: 4, z: 8, core: 2. Of those that a mesh axis runs over, the one named last changes fastest.
Arguments:
- inputs: bfloat16 [512, 16, 28672], P('tensor', None, 'store'), may hold values from -6 to 6
- out_grads: bfloat16 [512, 16, 8192], P('tensor', None, 'store'), may hold values from -6 to 6
- proj_in: bfloat16 [28672, 128], P('store'), may hold values from -0.03125 to 0.03125
- proj_out: bfloat16 [8192, 128], P('store'), may hold values from -0.125 to 0.125
- inv_fisher: float32 [16384, 16384], P('store', 'tensor'), may hold values from -1 to 4
- store_grads: float32 [8192, 16384], P('store', 'tensor'), may hold values from -0.005859375 to 0.005859375
Outputs:
- scores: float32 [512, 8192], P('tensor', 'store')
The draws below stay inside these ranges and needn't reach their ends.
All inputs are finite; a program needn't handle non-finite values.
Results may differ from the reference program's by a relative error of at most 0.0003.
Values sent between devices are 32-bit elements; how exact they have to be, the bound alone decides.
No kernel may reach another device: no remote copies, remote signals or barrier semaphores. Data moves between devices by JAX's collectives and lax.ppermute only.
A program may use at most 64 MiB of HBM per device.

```python
import math
import jax
import jax.numpy as jnp
from jax import lax

IN = 28672
OUT = 8192
PJ = 128
PK = 128
TOK = 16
EXAMPLES = 512
STORED = 8192
COORDS = 16384


def draw_inv_fisher(key, part):
    key_off = jax.random.fold_in(key, 11)
    key_diag = jax.random.fold_in(key, 12)
    coords = PK * PJ
    off_diag = jax.random.uniform(key_off, (coords, coords), jnp.float32, -0.9, 0.9)
    off_diag = off_diag / math.sqrt(coords)
    diag_values = 1.0 + 2.0 * jax.random.uniform(key_diag, (coords,), jnp.float32)
    positions = jnp.arange(coords)
    return off_diag.at[positions, positions].add(diag_values)


def with_spikes(array, own_key, source, target, shards_of, factor):
    owner, partner = [(jnp.arange(array.shape[axis_at]) // (array.shape[axis_at] // shards_of)).reshape([-1 if axis == axis_at else 1 for axis in range(array.ndim)]) for axis_at in (source, target)]
    chosen = jax.random.permutation(own_key, shards_of)[partner]
    strong = (owner == chosen) | (owner == (partner + shards_of // 2) % shards_of)
    return jnp.where(strong, factor * array, array)


def block_levels(stream_key, extent, cuts, least, largest):
    def one(axis_at, blocks):
        draws = jax.random.uniform(jax.random.fold_in(jax.random.fold_in(stream_key, 6), axis_at), (blocks,), jnp.float32, least / len(cuts), largest / len(cuts))
        return jnp.repeat(jnp.exp(draws), extent[axis_at] // blocks).reshape((-1,) + (1,) * (len(extent) - axis_at - 1))

    loudness = one(*cuts[0])
    for cut in cuts[1:]:
        loudness = loudness * one(*cut)
    return loudness


def scatter_about(rng, extent, deviation, reach, cuts=(), held_as=jnp.bfloat16):
    drawn = deviation * jax.random.normal(rng, extent, jnp.float32)
    if cuts:
        drawn = drawn * block_levels(rng, extent, cuts, -0.22, 0.18)
    return jnp.clip(drawn, -reach, reach).astype(held_as)


def bell_draw_with(rng, shape, scale, reach, cuts, heavy, dtype=jnp.bfloat16):
    drawn = scale * jax.random.normal(rng, shape, jnp.float32)
    if cuts:
        drawn = drawn * block_levels(rng, shape, cuts, -0.22, 0.18)
    return jnp.clip(with_spikes(drawn, jax.random.fold_in(rng, 3), *heavy), -reach, reach).astype(dtype)


def setup_inputs(seed: int = 0) -> dict:
    key_list = jax.random.split(jax.random.key(seed), 7)
    return {
        "inputs": scatter_about(key_list[0], (EXAMPLES, TOK, IN), 1.0, 6.0, ((0, 8), (2, 32))),
        "out_grads": scatter_about(key_list[1], (EXAMPLES, TOK, OUT), 1.0, 6.0, ((0, 8), (2, 32))),
        "proj_in": scatter_about(key_list[2], (IN, PJ), IN ** -0.5, 0.03125, ((0, 32),)),
        "proj_out": bell_draw_with(key_list[3], (OUT, PK), OUT ** -0.5, 0.125, ((0, 32),), (0, 1, 32, 2.75)),
        "inv_fisher": draw_inv_fisher(jax.random.fold_in(key_list[6], 71), 0),
        "store_grads": scatter_about(key_list[5], (STORED, COORDS), (64 * COORDS) ** -0.5, 0.005859375, ((0, 32), (1, 8)), jnp.float32),
    }


def reference(inputs, out_grads, proj_in, proj_out, inv_fisher, store_grads):
    act_proj = jnp.dot(inputs.reshape(EXAMPLES * TOK, IN), proj_in, preferred_element_type=jnp.float32).reshape(EXAMPLES, TOK, PJ)
    grad_proj = jnp.dot(out_grads.reshape(EXAMPLES * TOK, OUT), proj_out, preferred_element_type=jnp.float32).reshape(EXAMPLES, TOK, PK)
    joined = jnp.einsum("etk,etj->ekj", grad_proj.astype(jnp.float32), act_proj.astype(jnp.float32), precision=lax.Precision.HIGHEST)
    example_grads = joined.reshape(EXAMPLES, PK * PJ)
    preconditioned = jnp.dot(example_grads, inv_fisher, precision=lax.Precision.HIGHEST, preferred_element_type=jnp.float32)
    scores = lax.dot_general(preconditioned, store_grads, (((1,), (1,)), ((), ())), precision=lax.Precision.HIGHEST, preferred_element_type=jnp.float32)
    return scores
```

```python
import jax
import jax.numpy as jnp
from jax import lax
from jax.sharding import Mesh, PartitionSpec as P


HIGH = lax.Precision.HIGH
GROUPS = ((0, 1), (3, 2))


def shifted(array, axis, size, steps):
    if steps % size == 0:
        return array
    return lax.ppermute(array, axis, [(i, (i + steps) % size) for i in range(size)])


def summed_share(array, axis, size):
    pieces = lax.all_to_all(array.reshape(size, array.shape[0] // size, array.shape[1]), axis, 0, 0)
    return jnp.sum(pieces, axis=0)


def everyones(array, axis, size):
    copies = jnp.broadcast_to(array[None], (size,) + array.shape)
    return lax.all_to_all(copies, axis, 0, 0).reshape((size * array.shape[0],) + array.shape[1:])


def on_device(sizes, inputs, out_grads, proj_in, proj_out, inv_fisher, store_grads):
    ny, nz, nx = sizes["y"], sizes["z"], sizes["x"]
    examples, tokens = inputs.shape[0], inputs.shape[1]
    pj, pk = proj_in.shape[1], proj_out.shape[1]
    x = lax.axis_index("x")
    act_part = jnp.dot(inputs.reshape(examples * tokens, -1), proj_in, preferred_element_type=jnp.float32)
    grad_part = jnp.dot(out_grads.reshape(examples * tokens, -1), proj_out, preferred_element_type=jnp.float32)

    width = inv_fisher.shape[1] // nx

    def columns_for(array, k):
        return lax.dynamic_slice_in_dim(array, ((x + k) % nx) * width, width, 1)

    fisher = [shifted(columns_for(inv_fisher, k), "x", nx, k) for k in range(nx)]
    stored = [shifted(columns_for(store_grads, k), "x", nx, k) for k in range(nx)]

    both = jnp.concatenate([act_part, grad_part], axis=1)
    both = summed_share(both, "x", nx)
    both = summed_share(both, "z", nz)
    few = examples // (nx * nz)
    act = both[:, :pj].reshape(few, tokens, pj)
    grad = both[:, pj:].reshape(few, tokens, pk)
    local = jnp.einsum("etk,etj->ekj", grad, act, precision=lax.Precision.HIGHEST)
    local = local.reshape(few, nz, -1).transpose(1, 0, 2)
    coords = local.shape[2]
    mine = lax.all_to_all(local, "z", 0, 0).reshape(few * nz, coords)
    mine = everyones(mine, "x", nx)
    rows = coords // nx
    mine = jnp.concatenate(
        [lax.dynamic_slice_in_dim(mine, ((x - k) % nx) * rows, rows, 1) for k in range(nx)], axis=1
    )
    own = {d: shifted(mine, "y", ny, -d) for d in range(ny)}
    total = None
    for group in GROUPS:
        these = jnp.stack([own[d] for d in group])
        other = lax.ppermute(these, "core", [(0, 1), (1, 0)])
        these = jnp.stack([these, other]).reshape(-1, coords)
        part = jnp.dot(these, jnp.concatenate(fisher, axis=0), precision=HIGH, preferred_element_type=jnp.float32)
        whole = everyones(summed_share(part, "z", nz), "z", nz)
        scored = [
            lax.dot_general(
                whole, s, (((1,), (1,)), ((), ())), precision=HIGH, preferred_element_type=jnp.float32
            )
            for s in stored
        ]
        half = whole.shape[0] // 2
        swapped = lax.ppermute(jnp.stack([s[half:] for s in scored]), "core", [(0, 1), (1, 0)])
        summed = None
        for k in range(nx):
            back = shifted(scored[k][:half] + swapped[k], "x", nx, -k)
            summed = back if summed is None else summed + back
        for at, d in enumerate(group):
            home = shifted(summed[at * examples : (at + 1) * examples], "y", ny, d)
            total = home if total is None else total + home
    return total


def solution(mesh):
    sizes = {"y": 4, "core": 2, "z": 8, "x": 4}
    named = Mesh(mesh.devices.reshape(tuple(sizes.values())), tuple(sizes))
    tensor, store = ("y", "core"), ("z", "x")
    placed = (
        P(tensor, None, store),
        P(tensor, None, store),
        P(store, None),
        P(store, None),
        P(store, tensor),
        P(store, tensor),
    )

    def run(*args):
        return on_device(sizes, *args)

    return jax.shard_map(run, mesh=named, in_specs=placed, out_specs=P(tensor, store), check_vma=False)
```

```python
import jax
import jax.numpy as jnp
from jax import lax
from jax.sharding import Mesh, PartitionSpec as P


HIGH = lax.Precision.HIGH
SWAP = [(0, 1), (1, 0)]


def shifted(array, axis, size, steps):
    if steps % size == 0:
        return array
    return lax.ppermute(array, axis, [(i, (i + steps) % size) for i in range(size)])


def summed_share(array, axis, size):
    pieces = lax.all_to_all(array.reshape(size, array.shape[0] // size, array.shape[1]), axis, 0, 0)
    return jnp.sum(pieces, axis=0)


def everyones(array, axis, size):
    copies = jnp.broadcast_to(array[None], (size,) + array.shape)
    gathered = lax.all_to_all(copies, axis, 0, 0)
    return gathered.reshape((size * array.shape[0],) + array.shape[1:])


def on_device(sizes, inputs, out_grads, proj_in, proj_out, inv_fisher, store_grads):
    ny, nz, nx = sizes["y"], sizes["z"], sizes["x"]
    examples, tokens = inputs.shape[0], inputs.shape[1]
    pj, pk = proj_in.shape[1], proj_out.shape[1]
    x = lax.axis_index("x")
    act_part = jnp.dot(inputs.reshape(examples * tokens, -1), proj_in, preferred_element_type=jnp.float32)
    grad_part = jnp.dot(out_grads.reshape(examples * tokens, -1), proj_out, preferred_element_type=jnp.float32)

    width = inv_fisher.shape[1] // nx

    def spread(array):
        own, other = [], []
        for k in range(nx):
            piece = lax.dynamic_slice_in_dim(array, ((x + k) & (nx - 1)) * width, width, 1)
            piece = shifted(piece, "x", nx, k)
            own.append(piece)
            other.append(lax.ppermute(piece, "core", SWAP))
        return own, other

    fisher = spread(inv_fisher)
    stored = spread(store_grads)

    both = jnp.concatenate([act_part, grad_part], axis=1)
    both = summed_share(both, "x", nx)
    both = summed_share(both, "z", nz)
    few = examples // (nx * nz)
    act = both[:, :pj].reshape(few, tokens, pj)
    grad = both[:, pj:].reshape(few, tokens, pk)
    local = jnp.einsum("etk,etj->ekj", grad, act, precision=lax.Precision.HIGHEST)
    local = local.reshape(few, nz, -1).transpose(1, 0, 2)
    coords = local.shape[2]
    mine = lax.all_to_all(local, "z", 0, 0).reshape(few * nz, coords)
    mine = everyones(mine, "x", nx)
    rows = coords // nx
    mine = jnp.concatenate(
        [lax.dynamic_slice_in_dim(mine, ((x - k) & (nx - 1)) * rows, rows, 1) for k in range(nx)], axis=1
    )
    owned = []
    for d in range(ny):
        owned.append(shifted(mine, "y", ny, -d))
    these = jnp.concatenate(owned, axis=0)
    part = []
    for blocks in fisher:
        total = None
        for k in range(nx):
            term = jnp.dot(
                these[:, k * rows : (k + 1) * rows], blocks[k], precision=HIGH, preferred_element_type=jnp.float32
            )
            total = term if total is None else total + term
        part.append(total)
    part = jnp.concatenate(part, axis=1)
    whole = everyones(summed_share(part, "z", nz), "z", nz)
    summed = None
    for k in range(nx):
        scored = None
        for side, blocks in enumerate(stored):
            term = lax.dot_general(
                whole[:, side * width : (side + 1) * width],
                blocks[k],
                (((1,), (1,)), ((), ())),
                precision=HIGH,
                preferred_element_type=jnp.float32,
            )
            scored = term if scored is None else scored + term
        back = shifted(scored, "x", nx, -k)
        summed = back if summed is None else summed + back
    result = None
    for d in range(ny):
        home = shifted(summed[d * examples : (d + 1) * examples], "y", ny, d)
        result = home if result is None else result + home
    return result


def solution(mesh):
    sizes = {"y": 4, "core": 2, "z": 8, "x": 4}
    named = Mesh(mesh.devices.reshape(tuple(sizes.values())), tuple(sizes))
    tensor, store = ("y", "core"), ("z", "x")
    placed = (
        P(tensor, None, store),
        P(tensor, None, store),
        P(store, None),
        P(store, None),
        P(store, tensor),
        P(store, tensor),
    )

    def run(*args):
        return on_device(sizes, *args)

    return jax.shard_map(run, mesh=named, in_specs=placed, out_specs=P(tensor, store), check_vma=False)
```

```python
import jax
import jax.numpy as jnp
from jax import lax
from jax.experimental import pallas as pl
from jax.experimental.pallas import tpu as pltpu
from jax.sharding import Mesh, PartitionSpec as P


FETCH_ORDER = (0, 1, 3, 2)
f32, bf16 = jnp.float32, jnp.bfloat16
ANY = pl.BlockSpec(memory_space=pl.ANY)
WHOLE = pl.BlockSpec(memory_space=pltpu.VMEM)
SWAP = [(0, 1), (1, 0)]


def shifted(array, axis, size, steps):
    if steps % size == 0:
        return array
    return lax.ppermute(array, axis, [(i, (i + steps) % size) for i in range(size)])


def summed_share(array, axis, size):
    pieces = lax.all_to_all(array.reshape(size, array.shape[0] // size, array.shape[1]), axis, 0, 0)
    return jnp.sum(pieces, axis=0)


def everyones(array, axis, size):
    copies = jnp.broadcast_to(array[None], (size,) + array.shape)
    gathered = lax.all_to_all(copies, axis, 0, 0)
    return gathered.reshape((size * array.shape[0],) + array.shape[1:])


def halves(values):
    high = values.astype(bf16)
    return high, (values - high.astype(f32)).astype(bf16)


def product(left, right, dims):
    def dot(a, b):
        return lax.dot_general(a, b, (dims, ((), ())), preferred_element_type=f32)

    return dot(left[0], right[1]) + dot(left[1], right[0]) + dot(left[0], right[0])


def project(inputs, out_grads, proj_in, proj_out, steps):
    def kernel(inputs_ref, out_grads_ref, proj_in_ref, proj_out_ref, out_ref):
        pj = proj_in_ref.shape[1]
        out_ref[:, :pj] = jnp.dot(inputs_ref[...], proj_in_ref[...], preferred_element_type=f32)
        out_ref[:, pj:] = jnp.dot(out_grads_ref[...], proj_out_ref[...], preferred_element_type=f32)

    rows = inputs.shape[0] // steps
    columns = proj_in.shape[1] + proj_out.shape[1]

    def split(array):
        return pl.BlockSpec((rows, array.shape[1]), lambda i: (i, 0))

    def all_of(array):
        return pl.BlockSpec(array.shape, lambda i: (0, 0))

    return pl.pallas_call(
        kernel,
        grid=(steps,),
        in_specs=[split(inputs), split(out_grads), all_of(proj_in), all_of(proj_out)],
        out_specs=pl.BlockSpec((rows, columns), lambda i: (i, 0)),
        out_shape=jax.ShapeDtypeStruct((inputs.shape[0], columns), f32),
        name="project",
    )(inputs, out_grads, proj_in, proj_out)


def fetch(blocks, buffers, sems, i):
    return pltpu.make_async_copy(blocks[i], buffers.at[i], sems.at[i])


def precondition(owned, fisher, order):
    count, nx = len(owned), len(fisher[0])
    examples = owned[0].shape[0]
    rows, columns = fisher[0][0].shape

    def kernel(*refs):
        grads, blocks = refs[:count], refs[count : count + 2 * nx]
        out_ref, buffers, sems = refs[count + 2 * nx :]
        x = lax.axis_index("x")
        copies = [[fetch(blocks, buffers, sems, side * nx + k) for side in range(2)] for k in range(nx)]
        for k in order:
            for copy in copies[k]:
                copy.start()
        for at, k in enumerate(order):
            first = pl.multiple_of(((x - k) & (nx - 1)) * rows, rows)
            left = halves(jnp.concatenate([g[:, pl.ds(first, rows)] for g in grads], axis=0))
            for side in range(2):
                copies[k][side].wait()
                term = product(left, halves(buffers[side * nx + k]), ((1,), (0,)))
                where = slice(side * columns, (side + 1) * columns)
                if at:
                    out_ref[:, where] += term
                else:
                    out_ref[:, where] = term

    return pl.pallas_call(
        kernel,
        in_specs=[WHOLE] * count + [ANY] * (2 * nx),
        out_specs=WHOLE,
        out_shape=jax.ShapeDtypeStruct((count * examples, 2 * columns), f32),
        scratch_shapes=[pltpu.VMEM((2 * nx, rows, columns), f32), pltpu.SemaphoreType.DMA((2 * nx,))],
        name="precondition",
    )(*owned, *fisher[0], *fisher[1])


def score(whole, stored, ny):
    nx = len(stored[0])
    many, columns = stored[0][0].shape
    examples = whole.shape[0] // ny

    def kernel(*refs):
        whole_ref, blocks = refs[0], refs[1 : 1 + 2 * nx]
        out_ref, buffers, sems = refs[1 + 2 * nx :]
        x, y = lax.axis_index("x"), lax.axis_index("y")
        copies = [[fetch(blocks, buffers, sems, side * nx + k) for side in range(2)] for k in range(nx)]
        for pair in copies:
            for copy in pair:
                copy.start()
        left = [halves(whole_ref[:, side * columns : (side + 1) * columns]) for side in range(2)]
        for k in range(nx):
            for copy in copies[k]:
                copy.wait()
            total = None
            for side in range(2):
                term = product(left[side], halves(buffers[side * nx + k]), ((1,), (1,)))
                total = term if total is None else total + term
            for d in range(ny):
                place = ((y + d) & (ny - 1)) * nx + ((x - k) & (nx - 1))
                out_ref[place] = total[d * examples : (d + 1) * examples]

    return pl.pallas_call(
        kernel,
        in_specs=[WHOLE] + [ANY] * (2 * nx),
        out_specs=WHOLE,
        out_shape=jax.ShapeDtypeStruct((ny * nx, examples, many), f32),
        scratch_shapes=[pltpu.VMEM((2 * nx, many, columns), f32), pltpu.SemaphoreType.DMA((2 * nx,))],
        name="score",
    )(whole, *stored[0], *stored[1])


def on_device(sizes, inputs, out_grads, proj_in, proj_out, inv_fisher, store_grads):
    ny, nz, nx = sizes["y"], sizes["z"], sizes["x"]
    examples, tokens = inputs.shape[0], inputs.shape[1]
    pj, pk = proj_in.shape[1], proj_out.shape[1]
    x = lax.axis_index("x")

    width = inv_fisher.shape[1] // nx

    def spread(array):
        own, other = [], []
        for k in range(nx):
            piece = lax.dynamic_slice_in_dim(array, ((x + k) & (nx - 1)) * width, width, 1)
            piece = shifted(piece, "x", nx, k)
            own.append(piece)
            other.append(lax.ppermute(piece, "core", SWAP))
        return own, other

    fisher = spread(inv_fisher)
    stored = spread(store_grads)

    both = project(
        inputs.reshape(examples * tokens, -1), out_grads.reshape(examples * tokens, -1), proj_in, proj_out, nx
    )
    both = summed_share(both, "x", nx)
    both = summed_share(both, "z", nz)
    few = examples // (nx * nz)
    act = both[:, :pj].reshape(few, tokens, pj)
    grad = both[:, pj:].reshape(few, tokens, pk)
    local = jnp.einsum("etk,etj->ekj", grad, act, precision=lax.Precision.HIGHEST)
    local = local.reshape(few, nz, -1).transpose(1, 0, 2)
    coords = local.shape[2]
    mine = lax.all_to_all(local, "z", 0, 0).reshape(few * nz, coords)
    mine = everyones(mine, "x", nx)
    owned = []
    for d in range(ny):
        owned.append(shifted(mine, "y", ny, -d))
    part = precondition(owned, fisher, FETCH_ORDER)
    whole = everyones(summed_share(part, "z", nz), "z", nz)
    scores = score(whole, stored, ny)
    scores = lax.all_to_all(scores, ("y", "x"), 0, 0, tiled=True)
    return jnp.sum(scores, axis=0)


def solution(mesh):
    sizes = {"y": 4, "core": 2, "z": 8, "x": 4}
    named = Mesh(mesh.devices.reshape(tuple(sizes.values())), tuple(sizes))
    tensor, store = ("y", "core"), ("z", "x")
    placed = (
        P(tensor, None, store),
        P(tensor, None, store),
        P(store, None),
        P(store, None),
        P(store, tensor),
        P(store, tensor),
    )

    def run(*args):
        return on_device(sizes, *args)

    return jax.shard_map(run, mesh=named, in_specs=placed, out_specs=P(tensor, store), check_vma=False)
```

```python
import jax
import jax.numpy as jnp
from jax import lax
from jax.experimental import pallas as pl
from jax.experimental.pallas import tpu as pltpu
from jax.sharding import Mesh, PartitionSpec as P


SWAP = [(0, 1), (1, 0)]


def shifted(array, axis, size, steps):
    if steps % size == 0:
        return array
    return lax.ppermute(array, axis, [(i, (i + steps) % size) for i in range(size)])


def pieces_of(array, axis):
    return lax.all_to_all(array, axis, 0, 0)


def summed_share(array, axis, size):
    pieces = pieces_of(array.reshape(size, array.shape[0] // size, array.shape[1]), axis)
    return summed(pieces)


def summed(pieces):
    return jnp.sum(pieces, axis=0)


f32, bf16 = jnp.float32, jnp.bfloat16
WHOLE = pl.BlockSpec(memory_space=pltpu.VMEM)
ROOM = pltpu.CompilerParams(vmem_limit_bytes=24 * 2**20)


def near(array):
    return pltpu.with_memory_space_constraint(array, pltpu.VMEM)


def halves(values):
    high = values.astype(bf16)
    return high, (values - high.astype(f32)).astype(bf16)


def product(left, right, dims):
    def dot(a, b):
        return lax.dot_general(a, b, (dims, ((), ())), preferred_element_type=f32)

    return dot(left[0], right[1]) + dot(left[1], right[0]) + dot(left[0], right[0])


def project(inputs, out_grads, proj_in, proj_out, steps):
    def kernel(inputs_ref, out_grads_ref, proj_in_ref, proj_out_ref, out_ref):
        pj = proj_in_ref.shape[1]
        out_ref[:, :pj] = jnp.dot(inputs_ref[...], proj_in_ref[...], preferred_element_type=f32)
        out_ref[:, pj:] = jnp.dot(out_grads_ref[...], proj_out_ref[...], preferred_element_type=f32)

    rows = inputs.shape[0] // steps
    columns = proj_in.shape[1] + proj_out.shape[1]

    def split(array):
        return pl.BlockSpec((rows, array.shape[1]), lambda i: (i, 0))

    def all_of(array):
        return pl.BlockSpec(array.shape, lambda i: (0, 0))

    return pl.pallas_call(
        kernel,
        grid=(steps,),
        in_specs=[split(inputs), split(out_grads), all_of(proj_in), all_of(proj_out)],
        out_specs=pl.BlockSpec((rows, columns), lambda i: (i, 0)),
        out_shape=jax.ShapeDtypeStruct((inputs.shape[0], columns), f32),
        name="project",
        compiler_params=ROOM,
    )(inputs, out_grads, proj_in, proj_out)


def store_rows(out_ref, count, where, values, add):
    nz, columns = out_ref.shape[0], values.shape[1]
    values = values.reshape(count, nz, -1, columns)
    each = values.shape[2]
    for d in range(count):
        rows = slice(d * each, (d + 1) * each)
        if add:
            out_ref[:, rows, where] += values[d]
        else:
            out_ref[:, rows, where] = values[d]


def precondition(owned, fisher, nz):
    count, nx = len(owned), len(fisher[0])
    examples = owned[0].shape[0]
    rows, columns = fisher[0][0].shape

    def kernel(*refs):
        grads, blocks, out_ref = refs[:count], refs[count : count + 2 * nx], refs[count + 2 * nx]
        x = lax.axis_index("x")
        for k in range(nx):
            first = pl.multiple_of(((x - k) & (nx - 1)) * rows, rows)
            left = halves(jnp.concatenate([g[:, pl.ds(first, rows)] for g in grads], axis=0))
            for side in range(2):
                term = product(left, halves(blocks[side * nx + k][...]), ((1,), (0,)))
                store_rows(out_ref, count, slice(side * columns, (side + 1) * columns), term, k > 0)

    return pl.pallas_call(
        kernel,
        in_specs=[WHOLE] * (count + 2 * nx),
        out_specs=WHOLE,
        out_shape=pltpu.VMEM((nz, count * examples // nz, 2 * columns), f32),
        compiler_params=ROOM,
    )(*[near(g) for g in owned], *[near(f) for f in fisher[0] + fisher[1]])


def sum_copies(first, second):
    few, columns = first.shape
    nz, many = second.shape[:2]

    def kernel(first_ref, second_ref, out_ref):
        total = jnp.concatenate([first_ref[...], jnp.sum(second_ref[...], axis=0)], axis=0)
        for z in range(nz):
            out_ref[z] = total

    return pl.pallas_call(
        kernel,
        in_specs=[WHOLE] * 2,
        out_specs=WHOLE,
        out_shape=pltpu.VMEM((nz, few + many, columns), f32),
        name="sum_copies",
        compiler_params=ROOM,
    )(near(first), near(second))


def score(whole, stored, ny):
    nx = len(stored[0])
    many, columns = stored[0][0].shape
    nz = whole.shape[0]
    examples = nz * whole.shape[1] // ny

    def kernel(*refs):
        whole_ref, blocks = refs[0], refs[1 : 1 + 2 * nx]
        out_ref = refs[1 + 2 * nx]
        x, y = lax.axis_index("x"), lax.axis_index("y")
        left = []
        for side in range(2):
            values = whole_ref[:, :, side * columns : (side + 1) * columns]
            left.append(halves(values.reshape(ny * examples, columns)))
        for k in range(nx):
            total = None
            for side in range(2):
                term = product(left[side], halves(blocks[side * nx + k][...]), ((1,), (1,)))
                total = term if total is None else total + term
            total = total.reshape(nz, ny, examples // nz, many)
            for d in range(ny):
                place = ((y + d) & (ny - 1)) * nx + ((x - k) & (nx - 1))
                out_ref[place] = total[:, d].reshape(examples, many)

    return pl.pallas_call(
        kernel,
        in_specs=[WHOLE] * (1 + 2 * nx),
        out_specs=WHOLE,
        out_shape=pltpu.VMEM((ny * nx, examples, many), f32),
        name="score",
        compiler_params=ROOM,
    )(near(whole), *[near(s) for s in stored[0] + stored[1]])


def on_device(sizes, inputs, out_grads, proj_in, proj_out, inv_fisher, store_grads):
    ny, nz, nx = sizes["y"], sizes["z"], sizes["x"]
    examples, tokens = inputs.shape[0], inputs.shape[1]
    pj, pk = proj_in.shape[1], proj_out.shape[1]
    x = lax.axis_index("x")

    width = inv_fisher.shape[1] // nx

    def spread(array):
        own, other = [], []
        for k in range(nx):
            piece = lax.dynamic_slice_in_dim(array, ((x + k) & (nx - 1)) * width, width, 1)
            piece = shifted(piece, "x", nx, k)
            own.append(piece)
            other.append(lax.ppermute(piece, "core", SWAP))
        return own, other

    fisher = spread(inv_fisher)
    stored = spread(store_grads)

    both = project(
        inputs.reshape(examples * tokens, -1), out_grads.reshape(examples * tokens, -1), proj_in, proj_out, nx
    )
    both = summed_share(both, "x", nx)
    both = summed_share(both, "z", nz)
    few = examples // (nx * nz)
    act = both[:, :pj].reshape(few, tokens, pj)
    grad = both[:, pj:].reshape(few, tokens, pk)
    local = jnp.einsum("etk,etj->ekj", grad, act, precision=lax.Precision.HIGHEST)
    local = local.reshape(few, nz, -1).transpose(1, 0, 2)
    coords = local.shape[2]
    mine = pieces_of(local, "z").reshape(few * nz, coords)
    mine = pieces_of(jnp.broadcast_to(mine[None], (nx,) + mine.shape), "x")
    mine = mine.reshape(nx * few * nz, coords)
    owned = []
    for d in range(ny):
        owned.append(shifted(mine, "y", ny, -d))
    ahead = precondition(owned[:1], fisher, nz)
    ahead = summed(pieces_of(ahead, "z"))
    rest = precondition(owned[1:], fisher, nz)
    rest = pieces_of(rest, "z")
    whole = pieces_of(sum_copies(ahead, rest), "z")
    scores = pieces_of(score(whole, stored, ny), ("y", "x"))
    return jnp.sum(scores, axis=0)


def solution(mesh):
    sizes = {"y": 4, "core": 2, "z": 8, "x": 4}
    named = Mesh(mesh.devices.reshape(tuple(sizes.values())), tuple(sizes))
    tensor, store = ("y", "core"), ("z", "x")
    placed = (
        P(tensor, None, store),
        P(tensor, None, store),
        P(store, None),
        P(store, None),
        P(store, tensor),
        P(store, tensor),
    )

    def run(*args):
        return on_device(sizes, *args)

    return jax.shard_map(run, mesh=named, in_specs=placed, out_specs=P(tensor, store), check_vma=False)
```

```python
import jax
import jax.numpy as jnp
from jax import lax
from jax.experimental import pallas as pl
from jax.experimental.pallas import tpu as pltpu
from jax.sharding import Mesh, PartitionSpec as P


SWAP = [(0, 1), (1, 0)]


def shifted(array, axis, size, steps):
    if steps % size == 0:
        return array
    return lax.ppermute(array, axis, [(i, (i + steps) % size) for i in range(size)])


def pieces_of(array, axis):
    return lax.all_to_all(array, axis, 0, 0)


def summed_share(array, axis, size):
    pieces = pieces_of(array.reshape(size, array.shape[0] // size, array.shape[1]), axis)
    return summed(pieces)


def summed(pieces):
    return jnp.sum(pieces, axis=0)


f32, bf16 = jnp.float32, jnp.bfloat16
WHOLE = pl.BlockSpec(memory_space=pltpu.VMEM)
ROOM = pltpu.CompilerParams(vmem_limit_bytes=24 * 2**20)


def near(array):
    return pltpu.with_memory_space_constraint(array, pltpu.VMEM)


def halves(values):
    high = values.astype(bf16)
    return high, (values - high.astype(f32)).astype(bf16)


def product(left, right, dims):
    def dot(a, b):
        return lax.dot_general(a, b, (dims, ((), ())), preferred_element_type=f32)

    return dot(left[0], right[1]) + dot(left[1], right[0]) + dot(left[0], right[0])


def project(inputs, out_grads, proj_in, proj_out, steps):
    def kernel(inputs_ref, out_grads_ref, proj_in_ref, proj_out_ref, out_ref):
        pj = proj_in_ref.shape[1]
        out_ref[:, :pj] = jnp.dot(inputs_ref[...], proj_in_ref[...], preferred_element_type=f32)
        out_ref[:, pj:] = jnp.dot(out_grads_ref[...], proj_out_ref[...], preferred_element_type=f32)

    rows = inputs.shape[0] // steps
    columns = proj_in.shape[1] + proj_out.shape[1]

    def split(array):
        return pl.BlockSpec((rows, array.shape[1]), lambda i: (i, 0))

    def all_of(array):
        return pl.BlockSpec(array.shape, lambda i: (0, 0))

    return pl.pallas_call(
        kernel,
        grid=(steps,),
        in_specs=[split(inputs), split(out_grads), all_of(proj_in), all_of(proj_out)],
        out_specs=pl.BlockSpec((rows, columns), lambda i: (i, 0)),
        out_shape=jax.ShapeDtypeStruct((inputs.shape[0], columns), f32),
        name="project",
    )(inputs, out_grads, proj_in, proj_out)


def store_rows(out_ref, count, where, values, add):
    nz, columns = out_ref.shape[0], values.shape[1]
    values = values.reshape(count, nz, -1, columns)
    each = values.shape[2]
    for d in range(count):
        rows = slice(d * each, (d + 1) * each)
        if add:
            out_ref[:, rows, where] += values[d]
        else:
            out_ref[:, rows, where] = values[d]


def precondition(owned, fisher, nz):
    count, nx = len(owned), len(fisher[0])
    examples = owned[0].shape[0]
    rows, columns = fisher[0][0].shape

    def kernel(*refs):
        grads, blocks, out_ref = refs[:count], refs[count : count + 2 * nx], refs[count + 2 * nx]
        x = lax.axis_index("x")
        for k in range(nx):
            first = pl.multiple_of(((x - k) & (nx - 1)) * rows, rows)
            left = halves(jnp.concatenate([g[:, pl.ds(first, rows)] for g in grads], axis=0))
            for side in range(2):
                term = product(left, halves(blocks[side * nx + k][...]), ((1,), (0,)))
                store_rows(out_ref, count, slice(side * columns, (side + 1) * columns), term, k > 0)

    return pl.pallas_call(
        kernel,
        in_specs=[WHOLE] * (count + 2 * nx),
        out_specs=WHOLE,
        out_shape=pltpu.VMEM((nz, count * examples // nz, 2 * columns), f32),
        compiler_params=ROOM,
    )(*[near(g) for g in owned], *[near(f) for f in fisher[0] + fisher[1]])


def sum_copies(pieces):
    nz = pieces.shape[0]

    def kernel(pieces_ref, out_ref):
        total = jnp.sum(pieces_ref[...], axis=0)
        for z in range(nz):
            out_ref[z] = total

    return pl.pallas_call(
        kernel,
        in_specs=[WHOLE],
        out_specs=WHOLE,
        out_shape=pltpu.VMEM(pieces.shape, f32),
        name="sum_copies",
        compiler_params=ROOM,
    )(near(pieces))


def score(whole, stored, ny):
    nx = len(stored[0])
    many, columns = stored[0][0].shape
    nz = whole.shape[0]
    examples = nz * whole.shape[1] // ny

    def kernel(*refs):
        whole_ref, blocks = refs[0], refs[1 : 1 + 2 * nx]
        out_ref = refs[1 + 2 * nx]
        x, y = lax.axis_index("x"), lax.axis_index("y")
        left = []
        for side in range(2):
            values = whole_ref[:, :, side * columns : (side + 1) * columns]
            left.append(halves(values.reshape(ny * examples, columns)))
        for k in range(nx):
            total = None
            for side in range(2):
                term = product(left[side], halves(blocks[side * nx + k][...]), ((1,), (1,)))
                total = term if total is None else total + term
            total = total.reshape(nz, ny, examples // nz, many)
            for d in range(ny):
                place = ((y + d) & (ny - 1)) * nx + ((x - k) & (nx - 1))
                out_ref[place] = total[:, d].reshape(examples, many)

    return pl.pallas_call(
        kernel,
        in_specs=[WHOLE] * (1 + 2 * nx),
        out_specs=WHOLE,
        out_shape=pltpu.VMEM((ny * nx, examples, many), f32),
        name="score",
        compiler_params=ROOM,
    )(near(whole), *[near(s) for s in stored[0] + stored[1]])


def on_device(sizes, inputs, out_grads, proj_in, proj_out, inv_fisher, store_grads):
    ny, nz, nx = sizes["y"], sizes["z"], sizes["x"]
    examples, tokens = inputs.shape[0], inputs.shape[1]
    pj, pk = proj_in.shape[1], proj_out.shape[1]
    x = lax.axis_index("x")

    width = inv_fisher.shape[1] // nx

    def spread(array):
        own, other = [], []
        for k in range(nx):
            piece = lax.dynamic_slice_in_dim(array, ((x + k) & (nx - 1)) * width, width, 1)
            piece = shifted(piece, "x", nx, k)
            own.append(piece)
            other.append(lax.ppermute(piece, "core", SWAP))
        return own, other

    fisher = spread(inv_fisher)
    stored = spread(store_grads)

    both = project(
        inputs.reshape(examples * tokens, -1), out_grads.reshape(examples * tokens, -1), proj_in, proj_out, nx
    )
    both = summed_share(both, "x", nx)
    both = summed_share(both, "z", nz)
    few = examples // (nx * nz)
    act = both[:, :pj].reshape(few, tokens, pj)
    grad = both[:, pj:].reshape(few, tokens, pk)
    local = jnp.einsum("etk,etj->ekj", grad, act, precision=lax.Precision.HIGHEST)
    local = local.reshape(few, nz, -1).transpose(1, 0, 2)
    coords = local.shape[2]
    mine = pieces_of(local, "z").reshape(few * nz, coords)
    mine = pieces_of(jnp.broadcast_to(mine[None], (nx,) + mine.shape), "x")
    mine = mine.reshape(nx * few * nz, coords)
    owned = []
    for d in range(ny):
        owned.append(shifted(mine, "y", ny, -d))
    part = pieces_of(precondition(owned, fisher, nz), "z")
    whole = pieces_of(sum_copies(part), "z")
    scores = pieces_of(score(whole, stored, ny), ("y", "x"))
    return jnp.sum(scores, axis=0)


def solution(mesh):
    sizes = {"y": 4, "core": 2, "z": 8, "x": 4}
    named = Mesh(mesh.devices.reshape(tuple(sizes.values())), tuple(sizes))
    tensor, store = ("y", "core"), ("z", "x")
    placed = (
        P(tensor, None, store),
        P(tensor, None, store),
        P(store, None),
        P(store, None),
        P(store, tensor),
        P(store, tensor),
    )

    def run(*args):
        return on_device(sizes, *args)

    return jax.shard_map(run, mesh=named, in_specs=placed, out_specs=P(tensor, store), check_vma=False)
```

```python
import jax
import jax.numpy as jnp
from jax import lax
from jax.experimental import pallas as pl
from jax.experimental.pallas import tpu as pltpu
from jax.sharding import Mesh, PartitionSpec as P


SWAP = [(0, 1), (1, 0)]


def shifted(array, axis, size, steps):
    if steps % size == 0:
        return array
    return lax.ppermute(array, axis, [(i, (i + steps) % size) for i in range(size)])


def pieces_of(array, axis):
    return lax.all_to_all(array, axis, 0, 0)


def summed_share(array, axis, size):
    pieces = pieces_of(array.reshape(size, array.shape[0] // size, array.shape[1]), axis)
    return summed(pieces)


def summed(pieces):
    return jnp.sum(pieces, axis=0)


f32, bf16 = jnp.float32, jnp.bfloat16
WHOLE = pl.BlockSpec(memory_space=pltpu.VMEM)
ROOM = pltpu.CompilerParams(vmem_limit_bytes=24 * 2**20)


def near(array):
    return pltpu.with_memory_space_constraint(array, pltpu.VMEM)


def halves(values):
    high = values.astype(bf16)
    return high, (values - high.astype(f32)).astype(bf16)


def product(left, right, dims):
    def dot(a, b):
        return lax.dot_general(a, b, (dims, ((), ())), preferred_element_type=f32)

    return dot(left[0], right[1]) + dot(left[1], right[0]) + dot(left[0], right[0])


def project(inputs, out_grads, proj_in, proj_out, steps):
    def kernel(inputs_ref, out_grads_ref, proj_in_ref, proj_out_ref, out_ref):
        pj = proj_in_ref.shape[1]
        out_ref[:, :pj] = jnp.dot(inputs_ref[...], proj_in_ref[...], preferred_element_type=f32)
        out_ref[:, pj:] = jnp.dot(out_grads_ref[...], proj_out_ref[...], preferred_element_type=f32)

    rows = inputs.shape[0] // steps
    columns = proj_in.shape[1] + proj_out.shape[1]

    def split(array):
        return pl.BlockSpec((rows, array.shape[1]), lambda i: (i, 0))

    def all_of(array):
        return pl.BlockSpec(array.shape, lambda i: (0, 0))

    return pl.pallas_call(
        kernel,
        grid=(steps,),
        in_specs=[split(inputs), split(out_grads), all_of(proj_in), all_of(proj_out)],
        out_specs=pl.BlockSpec((rows, columns), lambda i: (i, 0)),
        out_shape=jax.ShapeDtypeStruct((inputs.shape[0], columns), f32),
        name="project",
    )(inputs, out_grads, proj_in, proj_out)


def store_rows(out_ref, count, where, values, add):
    nz, columns = out_ref.shape[0], values.shape[1]
    values = values.reshape(count, nz, -1, columns)
    each = values.shape[2]
    for d in range(count):
        rows = slice(d * each, (d + 1) * each)
        if add:
            out_ref[:, rows, where] += values[d]
        else:
            out_ref[:, rows, where] = values[d]


def precondition(owned, fisher, nz):
    count, nx = len(owned), len(fisher[0])
    examples = owned[0].shape[0]
    rows, columns = fisher[0][0].shape

    def kernel(*refs):
        grads, blocks, out_ref = refs[:count], refs[count : count + 2 * nx], refs[count + 2 * nx]
        x = lax.axis_index("x")
        for k in range(nx):
            first = pl.multiple_of(((x - k) & (nx - 1)) * rows, rows)
            left = halves(jnp.concatenate([g[:, pl.ds(first, rows)] for g in grads], axis=0))
            for side in range(2):
                term = product(left, halves(blocks[side * nx + k][...]), ((1,), (0,)))
                store_rows(out_ref, count, slice(side * columns, (side + 1) * columns), term, k > 0)

    return pl.pallas_call(
        kernel,
        in_specs=[WHOLE] * (count + 2 * nx),
        out_specs=WHOLE,
        out_shape=pltpu.VMEM((nz, count * examples // nz, 2 * columns), f32),
        compiler_params=ROOM,
    )(*[near(g) for g in owned], *[near(f) for f in fisher[0] + fisher[1]])


def sum_copies(pieces):
    nz = pieces.shape[0]

    def kernel(pieces_ref, out_ref):
        total = jnp.sum(pieces_ref[...], axis=0)
        for z in range(nz):
            out_ref[z] = total

    return pl.pallas_call(
        kernel,
        in_specs=[WHOLE],
        out_specs=WHOLE,
        out_shape=pltpu.VMEM(pieces.shape, f32),
        name="sum_copies",
        compiler_params=ROOM,
    )(near(pieces))


def split_sides(whole, columns):
    rows = whole.shape[0] * whole.shape[1]

    def kernel(whole_ref, *out_refs):
        for side in range(2):
            values = whole_ref[:, :, side * columns : (side + 1) * columns].reshape(rows, columns)
            out_refs[2 * side][...], out_refs[2 * side + 1][...] = halves(values)

    return pl.pallas_call(
        kernel,
        in_specs=[WHOLE],
        out_specs=[WHOLE] * 4,
        out_shape=[pltpu.VMEM((rows, columns), bf16)] * 4,
        name="split_sides",
        compiler_params=ROOM,
    )(near(whole))


def score(left, stored, ny, nz):
    nx = len(stored[0])
    many = stored[0][0].shape[0]
    examples = left[0].shape[0] // ny

    def kernel(*refs):
        lefts, blocks, out_ref = refs[:4], refs[4 : 4 + 2 * nx], refs[4 + 2 * nx]
        x, y = lax.axis_index("x"), lax.axis_index("y")
        for k in range(nx):
            total = None
            for side in range(2):
                pair = (lefts[2 * side][...], lefts[2 * side + 1][...])
                term = product(pair, halves(blocks[side * nx + k][...]), ((1,), (1,)))
                total = term if total is None else total + term
            total = total.reshape(nz, ny, examples // nz, many)
            for d in range(ny):
                place = ((y + d) & (ny - 1)) * nx + ((x - k) & (nx - 1))
                out_ref[place] = total[:, d].reshape(examples, many)

    return pl.pallas_call(
        kernel,
        in_specs=[WHOLE] * (4 + 2 * nx),
        out_specs=WHOLE,
        out_shape=pltpu.VMEM((ny * nx, examples, many), f32),
        name="score",
        compiler_params=ROOM,
    )(*[near(a) for a in left], *[near(s) for s in stored[0] + stored[1]])


def on_device(sizes, inputs, out_grads, proj_in, proj_out, inv_fisher, store_grads):
    ny, nz, nx = sizes["y"], sizes["z"], sizes["x"]
    examples, tokens = inputs.shape[0], inputs.shape[1]
    pj, pk = proj_in.shape[1], proj_out.shape[1]
    x = lax.axis_index("x")

    width = inv_fisher.shape[1] // nx

    def spread(array):
        own, other = [], []
        for k in range(nx):
            piece = lax.dynamic_slice_in_dim(array, ((x + k) & (nx - 1)) * width, width, 1)
            piece = shifted(piece, "x", nx, k)
            own.append(piece)
            other.append(lax.ppermute(piece, "core", SWAP))
        return own, other

    fisher = spread(inv_fisher)
    stored = spread(store_grads)

    both = project(
        inputs.reshape(examples * tokens, -1), out_grads.reshape(examples * tokens, -1), proj_in, proj_out, nx
    )
    both = summed_share(both, "x", nx)
    both = summed_share(both, "z", nz)
    few = examples // (nx * nz)
    act = both[:, :pj].reshape(few, tokens, pj)
    grad = both[:, pj:].reshape(few, tokens, pk)
    local = jnp.einsum("etk,etj->ekj", grad, act, precision=lax.Precision.HIGHEST)
    local = local.reshape(few, nz, -1).transpose(1, 0, 2)
    coords = local.shape[2]
    mine = pieces_of(local, "z").reshape(few * nz, coords)
    mine = pieces_of(jnp.broadcast_to(mine[None], (nx,) + mine.shape), "x")
    mine = mine.reshape(nx * few * nz, coords)
    owned = []
    for d in range(ny):
        owned.append(shifted(mine, "y", ny, -d))
    part = pieces_of(precondition(owned, fisher, nz), "z")
    whole = pieces_of(sum_copies(part), "z")
    scores = pieces_of(score(split_sides(whole, width), stored, ny, nz), ("y", "x"))
    return jnp.sum(scores, axis=0)


def solution(mesh):
    sizes = {"y": 4, "core": 2, "z": 8, "x": 4}
    named = Mesh(mesh.devices.reshape(tuple(sizes.values())), tuple(sizes))
    tensor, store = ("y", "core"), ("z", "x")
    placed = (
        P(tensor, None, store),
        P(tensor, None, store),
        P(store, None),
        P(store, None),
        P(store, tensor),
        P(store, tensor),
    )

    def run(*args):
        return on_device(sizes, *args)

    return jax.shard_map(run, mesh=named, in_specs=placed, out_specs=P(tensor, store), check_vma=False)
```

```python
import jax
import jax.numpy as jnp
from jax import lax
from jax.experimental import pallas as pl
from jax.experimental.pallas import tpu as pltpu
from jax.sharding import Mesh, PartitionSpec as P


SWAP = [(0, 1), (1, 0)]


def shifted(array, axis, size, steps):
    if steps % size == 0:
        return array
    return lax.ppermute(array, axis, [(i, (i + steps) % size) for i in range(size)])


def pieces_of(array, axis):
    return lax.all_to_all(array, axis, 0, 0)


def mirrored_pieces(array, size):
    groups = [list(range(size)), list(range(2 * size - 1, size - 1, -1))]
    return lax.all_to_all(array, ("core", "z"), 0, 0, axis_index_groups=groups)


def summed_share(array, axis, size):
    pieces = pieces_of(array.reshape(size, array.shape[0] // size, array.shape[1]), axis)
    return summed(pieces)


def summed(pieces):
    return jnp.sum(pieces, axis=0)


f32, bf16 = jnp.float32, jnp.bfloat16
WHOLE = pl.BlockSpec(memory_space=pltpu.VMEM)
ROOM = pltpu.CompilerParams(vmem_limit_bytes=24 * 2**20)


def near(array):
    return pltpu.with_memory_space_constraint(array, pltpu.VMEM)


def halves(values):
    high = values.astype(bf16)
    return high, (values - high.astype(f32)).astype(bf16)


def product(left, right, dims):
    def dot(a, b):
        return lax.dot_general(a, b, (dims, ((), ())), preferred_element_type=f32)

    return dot(left[0], right[1]) + dot(left[1], right[0]) + dot(left[0], right[0])


def project(inputs, out_grads, proj_in, proj_out, steps):
    def kernel(inputs_ref, out_grads_ref, proj_in_ref, proj_out_ref, out_ref):
        pj = proj_in_ref.shape[1]
        out_ref[:, :pj] = jnp.dot(inputs_ref[...], proj_in_ref[...], preferred_element_type=f32)
        out_ref[:, pj:] = jnp.dot(out_grads_ref[...], proj_out_ref[...], preferred_element_type=f32)

    rows = inputs.shape[0] // steps
    columns = proj_in.shape[1] + proj_out.shape[1]

    def split(array):
        return pl.BlockSpec((rows, array.shape[1]), lambda i: (i, 0))

    def all_of(array):
        return pl.BlockSpec(array.shape, lambda i: (0, 0))

    return pl.pallas_call(
        kernel,
        grid=(steps,),
        in_specs=[split(inputs), split(out_grads), all_of(proj_in), all_of(proj_out)],
        out_specs=pl.BlockSpec((rows, columns), lambda i: (i, 0)),
        out_shape=jax.ShapeDtypeStruct((inputs.shape[0], columns), f32),
        name="project",
    )(inputs, out_grads, proj_in, proj_out)


def store_rows(out_ref, count, where, values, add):
    nz, columns = out_ref.shape[0], values.shape[1]
    values = values.reshape(count, nz, -1, columns)
    each = values.shape[2]
    for d in range(count):
        rows = slice(d * each, (d + 1) * each)
        if add:
            out_ref[:, rows, where] += values[d]
        else:
            out_ref[:, rows, where] = values[d]


def precondition(owned, fisher, nz):
    count, nx = len(owned), len(fisher[0])
    examples = owned[0].shape[0]
    rows, columns = fisher[0][0].shape

    def kernel(*refs):
        grads, blocks, out_ref = refs[:count], refs[count : count + 2 * nx], refs[count + 2 * nx]
        x = lax.axis_index("x")
        for k in range(nx):
            first = pl.multiple_of(((x - k) & (nx - 1)) * rows, rows)
            left = halves(jnp.concatenate([g[:, pl.ds(first, rows)] for g in grads], axis=0))
            for side in range(2):
                term = product(left, halves(blocks[side * nx + k][...]), ((1,), (0,)))
                store_rows(out_ref, count, slice(side * columns, (side + 1) * columns), term, k > 0)

    return pl.pallas_call(
        kernel,
        in_specs=[WHOLE] * (count + 2 * nx),
        out_specs=WHOLE,
        out_shape=pltpu.VMEM((nz, count * examples // nz, 2 * columns), f32),
        compiler_params=ROOM,
    )(*[near(g) for g in owned], *[near(f) for f in fisher[0] + fisher[1]])


def sum_copies(pieces):
    nz = pieces.shape[0]

    def kernel(pieces_ref, out_ref):
        total = jnp.sum(pieces_ref[...], axis=0)
        for z in range(nz):
            out_ref[z] = total

    return pl.pallas_call(
        kernel,
        in_specs=[WHOLE],
        out_specs=WHOLE,
        out_shape=pltpu.VMEM(pieces.shape, f32),
        name="sum_copies",
        compiler_params=ROOM,
    )(near(pieces))


def split_sides(whole, columns):
    rows = whole.shape[0] * whole.shape[1]

    def kernel(whole_ref, *out_refs):
        for side in range(2):
            values = whole_ref[:, :, side * columns : (side + 1) * columns].reshape(rows, columns)
            out_refs[2 * side][...], out_refs[2 * side + 1][...] = halves(values)

    return pl.pallas_call(
        kernel,
        in_specs=[WHOLE],
        out_specs=[WHOLE] * 4,
        out_shape=[pltpu.VMEM((rows, columns), bf16)] * 4,
        name="split_sides",
        compiler_params=ROOM,
    )(near(whole))


def score(left, stored, ny, nz):
    nx = len(stored[0])
    many = stored[0][0].shape[0]
    examples = left[0].shape[0] // ny

    def kernel(*refs):
        lefts, blocks, out_ref = refs[:4], refs[4 : 4 + 2 * nx], refs[4 + 2 * nx]
        x, y = lax.axis_index("x"), lax.axis_index("y")
        for k in range(nx):
            total = None
            for side in range(2):
                pair = (lefts[2 * side][...], lefts[2 * side + 1][...])
                term = product(pair, halves(blocks[side * nx + k][...]), ((1,), (1,)))
                total = term if total is None else total + term
            total = total.reshape(nz, ny, examples // nz, many)
            for d in range(ny):
                place = ((y + d) & (ny - 1)) * nx + ((x - k) & (nx - 1))
                out_ref[place] = total[:, d].reshape(examples, many)

    return pl.pallas_call(
        kernel,
        in_specs=[WHOLE] * (4 + 2 * nx),
        out_specs=WHOLE,
        out_shape=pltpu.VMEM((ny * nx, examples, many), f32),
        name="score",
        compiler_params=ROOM,
    )(*[near(a) for a in left], *[near(s) for s in stored[0] + stored[1]])


def on_device(sizes, inputs, out_grads, proj_in, proj_out, inv_fisher, store_grads):
    ny, nz, nx = sizes["y"], sizes["z"], sizes["x"]
    examples, tokens = inputs.shape[0], inputs.shape[1]
    pj, pk = proj_in.shape[1], proj_out.shape[1]
    x = lax.axis_index("x")

    width = inv_fisher.shape[1] // nx

    def spread(array):
        own, other = [], []
        for k in range(nx):
            piece = lax.dynamic_slice_in_dim(array, ((x + k) & (nx - 1)) * width, width, 1)
            piece = shifted(piece, "x", nx, k)
            own.append(piece)
            other.append(lax.ppermute(piece, "core", SWAP))
        return own, other

    fisher = spread(inv_fisher)
    stored = spread(store_grads)

    both = project(
        inputs.reshape(examples * tokens, -1), out_grads.reshape(examples * tokens, -1), proj_in, proj_out, nx
    )
    both = summed_share(both, "x", nx)
    both = summed_share(both, "z", nz)
    few = examples // (nx * nz)
    act = both[:, :pj].reshape(few, tokens, pj)
    grad = both[:, pj:].reshape(few, tokens, pk)
    local = jnp.einsum("etk,etj->ekj", grad, act, precision=lax.Precision.HIGHEST)
    local = local.reshape(few, nz, -1).transpose(1, 0, 2)
    coords = local.shape[2]
    mine = pieces_of(local, "z").reshape(few * nz, coords)
    mine = pieces_of(jnp.broadcast_to(mine[None], (nx,) + mine.shape), "x")
    mine = mine.reshape(nx * few * nz, coords)
    owned = []
    for d in range(ny):
        owned.append(shifted(mine, "y", ny, -d))
    part = mirrored_pieces(precondition(owned, fisher, nz), nz)
    whole = mirrored_pieces(sum_copies(part), nz)
    scores = pieces_of(score(split_sides(whole, width), stored, ny, nz), ("y", "x"))
    return jnp.sum(scores, axis=0)


def solution(mesh):
    sizes = {"y": 4, "core": 2, "z": 8, "x": 4}
    named = Mesh(mesh.devices.reshape(tuple(sizes.values())), tuple(sizes))
    tensor, store = ("y", "core"), ("z", "x")
    placed = (
        P(tensor, None, store),
        P(tensor, None, store),
        P(store, None),
        P(store, None),
        P(store, tensor),
        P(store, tensor),
    )

    def run(*args):
        return on_device(sizes, *args)

    return jax.shard_map(run, mesh=named, in_specs=placed, out_specs=P(tensor, store), check_vma=False)
```

```python
import jax
import jax.numpy as jnp
from jax import lax
from jax.experimental import pallas as pl
from jax.experimental.pallas import tpu as pltpu
from jax.sharding import Mesh, PartitionSpec as P


SWAP = [(0, 1), (1, 0)]


def shifted(array, axis, size, steps):
    if steps % size == 0:
        return array
    return lax.ppermute(array, axis, [(i, (i + steps) % size) for i in range(size)])


def pieces_of(array, axis):
    return lax.all_to_all(array, axis, 0, 0)


def alternate_pieces(array, size):
    groups = []
    for parity in range(2):
        first = list(range(parity, size, 2))
        groups += [first, [size + i for i in reversed(first)]]
    return lax.all_to_all(array, ("core", "z"), 0, 0, axis_index_groups=groups)


def summed_share(array, axis, size):
    pieces = pieces_of(array.reshape(size, array.shape[0] // size, array.shape[1]), axis)
    return summed(pieces)


def summed(pieces):
    return jnp.sum(pieces, axis=0)


f32, bf16 = jnp.float32, jnp.bfloat16
WHOLE = pl.BlockSpec(memory_space=pltpu.VMEM)
ROOM = pltpu.CompilerParams(vmem_limit_bytes=24 * 2**20)


def near(array):
    return pltpu.with_memory_space_constraint(array, pltpu.VMEM)


def halves(values):
    high = values.astype(bf16)
    return high, (values - high.astype(f32)).astype(bf16)


def product(left, right, dims):
    def dot(a, b):
        return lax.dot_general(a, b, (dims, ((), ())), preferred_element_type=f32)

    return dot(left[0], right[1]) + dot(left[1], right[0]) + dot(left[0], right[0])


def project(inputs, out_grads, proj_in, proj_out, steps):
    def kernel(inputs_ref, out_grads_ref, proj_in_ref, proj_out_ref, out_ref):
        pj = proj_in_ref.shape[1]
        out_ref[:, :pj] = jnp.dot(inputs_ref[...], proj_in_ref[...], preferred_element_type=f32)
        out_ref[:, pj:] = jnp.dot(out_grads_ref[...], proj_out_ref[...], preferred_element_type=f32)

    rows = inputs.shape[0] // steps
    columns = proj_in.shape[1] + proj_out.shape[1]

    def split(array):
        return pl.BlockSpec((rows, array.shape[1]), lambda i: (i, 0))

    def all_of(array):
        return pl.BlockSpec(array.shape, lambda i: (0, 0))

    return pl.pallas_call(
        kernel,
        grid=(steps,),
        in_specs=[split(inputs), split(out_grads), all_of(proj_in), all_of(proj_out)],
        out_specs=pl.BlockSpec((rows, columns), lambda i: (i, 0)),
        out_shape=jax.ShapeDtypeStruct((inputs.shape[0], columns), f32),
        name="project",
    )(inputs, out_grads, proj_in, proj_out)


def precondition(owned, fisher, nz):
    count, nx = len(owned), len(fisher[0])
    each = owned[0].shape[0] // nz
    rows, columns = fisher[0][0].shape

    def kernel(*refs):
        grads, blocks = refs[:count], refs[count : count + 2 * nx]
        same_ref, down_ref, up_ref, total_ref = refs[count + 2 * nx :]
        x, parity = lax.axis_index("x"), lax.axis_index("z") & 1
        for k in range(nx):
            first = pl.multiple_of(((x - k) & (nx - 1)) * rows, rows)
            left = halves(jnp.concatenate([g[:, pl.ds(first, rows)] for g in grads], axis=0))
            for side in range(2):
                term = product(left, halves(blocks[side * nx + k][...]), ((1,), (0,)))
                term = term.reshape(count, nz, each, columns)
                where = slice(side * columns, (side + 1) * columns)
                for d in range(count):
                    if k:
                        total_ref[:, d * each : (d + 1) * each, where] += term[d]
                    else:
                        total_ref[:, d * each : (d + 1) * each, where] = term[d]
        for i in range(nz // 2):
            same_ref[i] = total_ref[2 * i + parity]
            other = total_ref[2 * i + 1 - parity]
            down_ref[i] = other[:, :columns]
            up_ref[i] = other[:, columns:]

    def out(width):
        return pltpu.VMEM((nz // 2, count * each, width), f32)

    return pl.pallas_call(
        kernel,
        in_specs=[WHOLE] * (count + 2 * nx),
        out_specs=[WHOLE] * 3,
        out_shape=[out(2 * columns), out(columns), out(columns)],
        scratch_shapes=[pltpu.VMEM((nz, count * each, 2 * columns), f32)],
        name="precondition",
        compiler_params=ROOM,
    )(*[near(g) for g in owned], *[near(f) for f in fisher[0] + fisher[1]])


def join(same, first, second):
    columns = first.shape[2]

    def kernel(same_ref, first_ref, second_ref, out_ref):
        out_ref[:, :, :columns] = same_ref[:, :, :columns] + first_ref[...]
        out_ref[:, :, columns:] = same_ref[:, :, columns:] + second_ref[...]

    return pl.pallas_call(
        kernel,
        in_specs=[WHOLE] * 3,
        out_specs=WHOLE,
        out_shape=pltpu.VMEM(same.shape, f32),
        name="join",
        compiler_params=ROOM,
    )(near(same), near(first), near(second))


def sum_copies(pieces):
    nz = pieces.shape[0]

    def kernel(pieces_ref, out_ref):
        total = jnp.sum(pieces_ref[...], axis=0)
        for z in range(nz):
            out_ref[z] = total

    return pl.pallas_call(
        kernel,
        in_specs=[WHOLE],
        out_specs=WHOLE,
        out_shape=pltpu.VMEM(pieces.shape, f32),
        name="sum_copies",
        compiler_params=ROOM,
    )(near(pieces))


def cut_sides(whole):
    columns = whole.shape[2] // 2

    def kernel(whole_ref, first_ref, second_ref):
        first_ref[...] = whole_ref[:, :, :columns]
        second_ref[...] = whole_ref[:, :, columns:]

    return pl.pallas_call(
        kernel,
        in_specs=[WHOLE],
        out_specs=[WHOLE] * 2,
        out_shape=[pltpu.VMEM(whole.shape[:2] + (columns,), f32)] * 2,
        name="cut_sides",
        compiler_params=ROOM,
    )(near(whole))


def score(same, other, stored, ny):
    nx = len(stored[0])
    many = stored[0][0].shape[0]
    half, each, columns = same[0].shape[0], same[0].shape[1] // ny, same[0].shape[2]
    rows = half * ny * each

    def kernel(*refs):
        parts, blocks, out_ref = refs[:4], refs[4 : 4 + 2 * nx], refs[4 + 2 * nx]
        x, y, parity = lax.axis_index("x"), lax.axis_index("y"), lax.axis_index("z") & 1
        left = []
        for side in range(2):
            pair = [parts[side][...].reshape(rows, columns), parts[2 + side][...].reshape(rows, columns)]
            left.append(halves(jnp.concatenate(pair, axis=0)))
        for k in range(nx):
            total = None
            for side in range(2):
                term = product(left[side], halves(blocks[side * nx + k][...]), ((1,), (1,)))
                total = term if total is None else total + term
            total = total.reshape(2, half, ny, each, many)
            for d in range(ny):
                place = ((y + d) & (ny - 1)) * nx + ((x - k) & (nx - 1))
                for i in range(half):
                    for group, z in enumerate((2 * i + parity, 2 * i + 1 - parity)):
                        out_ref[place, pl.ds(pl.multiple_of(z * each, each), each), :] = total[group, i, d]

    return pl.pallas_call(
        kernel,
        in_specs=[WHOLE] * (4 + 2 * nx),
        out_specs=WHOLE,
        out_shape=pltpu.VMEM((ny * nx, 2 * half * each, many), f32),
        name="score",
        compiler_params=ROOM,
    )(*[near(a) for a in same + other], *[near(s) for s in stored[0] + stored[1]])


def on_device(sizes, inputs, out_grads, proj_in, proj_out, inv_fisher, store_grads):
    ny, nz, nx = sizes["y"], sizes["z"], sizes["x"]
    examples, tokens = inputs.shape[0], inputs.shape[1]
    pj, pk = proj_in.shape[1], proj_out.shape[1]
    x = lax.axis_index("x")

    width = inv_fisher.shape[1] // nx

    def spread(array):
        own, other = [], []
        for k in range(nx):
            piece = lax.dynamic_slice_in_dim(array, ((x + k) & (nx - 1)) * width, width, 1)
            piece = shifted(piece, "x", nx, k)
            own.append(piece)
            other.append(lax.ppermute(piece, "core", SWAP))
        return own, other

    fisher = spread(inv_fisher)
    stored = spread(store_grads)

    both = project(
        inputs.reshape(examples * tokens, -1), out_grads.reshape(examples * tokens, -1), proj_in, proj_out, 2
    )
    both = summed_share(both, "x", nx)
    both = summed_share(both, "z", nz)
    few = examples // (nx * nz)
    act = both[:, :pj].reshape(few, tokens, pj)
    grad = both[:, pj:].reshape(few, tokens, pk)
    local = jnp.einsum("etk,etj->ekj", grad, act, precision=lax.Precision.HIGHEST)
    local = local.reshape(few, nz, -1).transpose(1, 0, 2)
    coords = local.shape[2]
    mine = pieces_of(local, "z").reshape(few * nz, coords)
    mine = pieces_of(jnp.broadcast_to(mine[None], (nx,) + mine.shape), "x")
    mine = mine.reshape(nx * few * nz, coords)
    owned = []
    for d in range(ny):
        owned.append(shifted(mine, "y", ny, -d))
    same, down, up = precondition(owned, fisher, nz)
    down, up = shifted(down, "z", nz, -1), shifted(up, "z", nz, 1)
    part = alternate_pieces(join(same, down, up), nz)
    same = cut_sides(alternate_pieces(sum_copies(part), nz))
    other = [shifted(same[0], "z", nz, 1), shifted(same[1], "z", nz, -1)]
    scores = pieces_of(score(list(same), other, stored, ny), ("y", "x"))
    return jnp.sum(scores, axis=0)


def solution(mesh):
    sizes = {"y": 4, "core": 2, "z": 8, "x": 4}
    named = Mesh(mesh.devices.reshape(tuple(sizes.values())), tuple(sizes))
    tensor, store = ("y", "core"), ("z", "x")
    placed = (
        P(tensor, None, store),
        P(tensor, None, store),
        P(store, None),
        P(store, None),
        P(store, tensor),
        P(store, tensor),
    )

    def run(*args):
        return on_device(sizes, *args)

    return jax.shard_map(run, mesh=named, in_specs=placed, out_specs=P(tensor, store), check_vma=False)
```
